128 devices in a mesh: seq: 16 (over x, y), chan: 8 (over z, core).
Axes of the slice: x: 4, y: 4, z: 4, core: 2. Of those that a mesh axis runs over, the one named last changes fastest.
Arguments:
- features: bfloat16 [768, 16384], P('chan', 'seq'), may hold values from -6 to 6
- weight_first: bfloat16 [5, 768, 768], P(None, 'chan'), may hold values from -0.09375 to 0.09375
- weight_widen: bfloat16 [1536, 768], P('chan'), may hold values from -0.21875 to 0.21875
- weight_second: bfloat16 [5, 1536, 1536], P(None, 'chan'), may hold values from -0.0625 to 0.0625
- weight_third: bfloat16 [5, 1536, 1536], P(None, 'chan'), may hold values from -0.0625 to 0.0625
- upstream: bfloat16 [1536, 8192], P('chan', 'seq'), may hold values from -6 to 6
Outputs:
- grad_features: bfloat16 [768, 16384], P('chan', 'seq')
- grad_first: float32 [5, 768, 768], P(None, 'seq', 'chan')
- grad_widen: float32 [768, 1536], P('seq', 'chan')
- grad_second: float32 [5, 1536, 1536], P(None, 'seq', 'chan')
- grad_third: float32 [5, 1536, 1536], P(None, 'seq', 'chan')
The draws below stay inside these ranges and needn't reach their ends.
All inputs are finite; a program needn't handle non-finite values.
Results may differ from the reference program's by a relative error of at most 0.038.
Values may be sent and summed in bfloat16 or wider, within the bound.
No kernel may reach another device: no remote copies, remote signals or barrier semaphores. Data moves between devices by JAX's collectives and lax.ppermute only.
A program may use at most 128 MiB of HBM per device.

```python
import math
import jax
import jax.numpy as jnp
from jax import lax

C0 = 768
C1 = 1536
KW = 5
POS = 16384
HALF = 8192
N_CHAN = 8


def level_of(stream_key, shape, shards, smallest, high):
    gain, own = 1.0, jax.random.fold_in(stream_key, 6)
    for dim, parts in shards:
        steps = jnp.exp(jax.random.uniform(jax.random.fold_in(own, dim), (parts,), jnp.float32, smallest / len(shards), high / len(shards)))
        gain = gain * jnp.repeat(steps, shape[dim] // parts).reshape([-1 if axis == dim else 1 for axis in range(len(shape))])
    return gain


def bell_draw(rng, extent, width, limit, split=(), held_as=jnp.bfloat16):
    drawn = width * jax.random.normal(rng, extent, jnp.float32)
    if split:
        drawn = drawn * level_of(rng, extent, split, -0.22, 0.18)
    return jnp.clip(drawn, -limit, limit).astype(held_as)


def setup_inputs(seed: int = 0) -> dict:
    seeds = jax.random.split(jax.random.key(seed), 7)
    return {
        "features": bell_draw(seeds[0], (C0, POS), 1.0, 6.0, ((0, 8), (1, 16))),
        "weight_first": bell_draw(seeds[1], (KW, C0, C0), (KW * C0) ** -0.5, 0.09375, ((1, 8),)),
        "weight_widen": bell_draw(seeds[2], (C1, C0), C0 ** -0.5, 0.21875, ((0, 8),)),
        "weight_second": bell_draw(seeds[3], (KW, C1, C1), (KW * C1) ** -0.5, 0.0625, ((1, 8),)),
        "weight_third": bell_draw(seeds[4], (KW, C1, C1), (KW * C1) ** -0.5, 0.0625, ((1, 8),)),
        "upstream": bell_draw(seeds[5], (C1, HALF), 1.0, 6.0, ((0, 8), (1, 16))),
    }


EPSILON = 1e-06
ROOT_HALF = 0.7071067811865476
DENSITY_SCALE = 0.3989422804014327

def gelu_exact(values):
    return 0.5 * values * (1.0 + lax.erf(values * ROOT_HALF))

def gelu_slope(values):
    return 0.5 * (1.0 + lax.erf(values * ROOT_HALF)) + values * DENSITY_SCALE * jnp.exp(-0.5 * values * values)

def norm_factor(values):
    return lax.rsqrt(lax.optimization_barrier(jnp.mean(values * values, axis=0)) + EPSILON)

def activate(gathered):
    values = gathered.astype(jnp.float32)
    factor = norm_factor(values)
    return (factor, gelu_exact(values * factor[None, :]).astype(jnp.bfloat16))

def conv_cols(padded, weight, length):
    total = jnp.dot(weight[0], padded[:, 0:length], preferred_element_type=jnp.float32)
    for offset in range(1, weight.shape[0]):
        total = total + jnp.dot(weight[offset], padded[:, offset:offset + length], preferred_element_type=jnp.float32)
    return total

def contract_rows(left, right):
    return lax.dot_general(left, right, (((0,), (0,)), ((), ())), preferred_element_type=jnp.float32)

def contract_cols(left, right):
    return lax.dot_general(left, right, (((1,), (1,)), ((), ())), preferred_element_type=jnp.float32)

def pad_cols(values):
    return jnp.pad(values, ((0, 0), (2, 2)))

def norm_back(grad_acts, gathered, factor):
    values = gathered.astype(jnp.float32)
    grad_normed = grad_acts * gelu_slope(values * factor[None, :])
    col_sums = lax.optimization_barrier(jnp.sum(grad_normed * values, axis=0))
    cubed = factor * factor * factor
    return factor[None, :] * grad_normed - values * (cubed * col_sums / values.shape[0])[None, :]

def block_back(grad_out, gathered, factor, padded, weight, grad_scale):
    length = grad_out.shape[1]
    width_full = weight.shape[2]
    grad_low = grad_out.astype(jnp.bfloat16)
    tap_terms = jnp.stack([contract_cols(padded[:, offset:offset + length], grad_low) for offset in range(weight.shape[0])]) * grad_scale
    group_width = weight.shape[1] // N_CHAN
    spread = pad_cols(grad_low)

    def add_group(group, total):
        start = (group * group_width).astype(jnp.int32)
        rows = lax.dynamic_slice_in_dim(spread, start, group_width, 0)
        weight_rows = lax.dynamic_slice_in_dim(weight, start, group_width, 1)
        partial_value = contract_rows(weight_rows[0], rows[:, 4:4 + length])
        for offset in range(1, weight.shape[0]):
            partial_value = partial_value + contract_rows(weight_rows[offset], rows[:, 4 - offset:4 - offset + length])
        rounded = lax.optimization_barrier(partial_value.astype(jnp.bfloat16))
        return total + rounded.astype(jnp.float32)
    grad_acts = lax.fori_loop(0, N_CHAN, add_group, jnp.zeros((width_full, length), jnp.float32))
    return (norm_back(grad_acts, gathered, factor), tap_terms)

def reference(features, weight_first, weight_widen, weight_second, weight_third, upstream):
    grad_scale = 1.0 / math.sqrt(POS)
    factor_a, acts_a = activate(features)
    padded_a = pad_cols(acts_a)
    mixed_a = (features.astype(jnp.float32) + conv_cols(padded_a, weight_first, POS)).astype(jnp.bfloat16)
    pooled = (mixed_a.astype(jnp.float32).reshape(C0, HALF, 2).sum(axis=2) * 0.5).astype(jnp.bfloat16)
    widened = jnp.dot(weight_widen, pooled, preferred_element_type=jnp.float32).astype(jnp.bfloat16)
    factor_b, acts_b = activate(widened)
    padded_b = pad_cols(acts_b)
    mixed_b = (widened.astype(jnp.float32) + conv_cols(padded_b, weight_second, HALF)).astype(jnp.bfloat16)
    factor_c, acts_c = activate(mixed_b)
    padded_c = pad_cols(acts_c)
    grad_run = upstream.astype(jnp.float32)
    grad_step, grad_third = block_back(grad_run, mixed_b, factor_c, padded_c, weight_third, grad_scale)
    grad_run = grad_run + grad_step
    grad_step, grad_second = block_back(grad_run, widened, factor_b, padded_b, weight_second, grad_scale)
    grad_run = grad_run + grad_step
    top_low = grad_run.astype(jnp.bfloat16)
    grad_widen = contract_cols(pooled, top_low) * grad_scale
    group_width = C1 // N_CHAN

    def add_group(group, total):
        start = (group * group_width).astype(jnp.int32)
        rows = lax.dynamic_slice_in_dim(top_low, start, group_width, 0)
        weight_rows = lax.dynamic_slice_in_dim(weight_widen, start, group_width, 0)
        rounded = lax.optimization_barrier(contract_rows(weight_rows, rows).astype(jnp.bfloat16))
        return total + rounded.astype(jnp.float32)
    grad_pooled = lax.fori_loop(0, N_CHAN, add_group, jnp.zeros((C0, HALF), jnp.float32))
    grad_mixed = jnp.broadcast_to((grad_pooled * 0.5)[:, :, None], (C0, HALF, 2)).reshape(C0, POS)
    grad_step, grad_first = block_back(grad_mixed, features, factor_a, padded_a, weight_first, grad_scale)
    grad_features = (grad_mixed + grad_step).astype(jnp.bfloat16)
    return (grad_features, grad_first, grad_widen, grad_second, grad_third)
```

```python
import math

import jax
import jax.numpy as jnp
from jax import lax
from jax.sharding import Mesh
from jax.sharding import PartitionSpec as P

EPSILON = 1e-06
ROOT_HALF = 0.7071067811865476
DENSITY_SCALE = 0.3989422804014327
BF = jnp.bfloat16
F32 = jnp.float32
SEQ = ("x", "y", "core")


def gelu_pair(s):
    half_erf = 0.5 * (1.0 + lax.erf(s * ROOT_HALF))
    return s * half_erf, half_erf + s * DENSITY_SCALE * jnp.exp(-0.5 * s * s)


def rot(block, axis, step):
    count = lax.axis_size(axis)
    return lax.ppermute(block, axis, [(i, (i + step) % count) for i in range(count)])


def swap(block):
    return lax.ppermute(block, "core", [(0, 1), (1, 0)])


def halo(block):
    count = math.prod(lax.axis_size(a) for a in SEQ)
    up = [(i, i + 1) for i in range(count - 1)]
    low = lax.ppermute(block[:, -2:], SEQ, up)
    high = lax.ppermute(block[:, :2], SEQ, [(b, a) for a, b in up])
    return jnp.concatenate([low, block, high], axis=1)


def mm(left, right):
    return jnp.dot(left, right, preferred_element_type=F32)


def mm_rows(left, right):
    return lax.dot_general(left, right, (((0,), (0,)), ((), ())), preferred_element_type=F32)


def mm_cols(left, right):
    return lax.dot_general(left, right, (((1,), (1,)), ((), ())), preferred_element_type=F32)


def by_core(core, own, other, axis=0):
    return jnp.where(
        core == 0,
        jnp.concatenate([own, other], axis=axis),
        jnp.concatenate([other, own], axis=axis),
    )


def fine(block, core):
    half = block.shape[1] // 2
    own = lax.dynamic_slice_in_dim(block, core * half, half, 1)
    other = lax.dynamic_slice_in_dim(block, (1 - core) * half, half, 1)
    return by_core(core, own, swap(other))


def turn(weight, z):
    width = weight.shape[-1] // 4
    twice = jnp.concatenate([weight, weight], axis=-1)
    return lax.dynamic_slice_in_dim(twice, z * width, 4 * width, weight.ndim - 1)


def gather_z(block):
    return jnp.concatenate([block] + [rot(block, "z", -j) for j in (1, 2, 3)], axis=0)


def activate(gathered):
    values = gathered.astype(F32)
    factor = lax.rsqrt(jnp.mean(values * values, axis=0, keepdims=True) + EPSILON)
    act, slope = gelu_pair(values * factor)
    return factor, act.astype(BF), slope * values


def conv(padded, weights, length, core):
    outs = []
    for weight in weights:
        total = mm(weight[0], padded[:, 0:length])
        for k in range(1, weight.shape[0]):
            total = total + mm(weight[k], padded[:, k : k + length])
        outs.append(total)
    return by_core(core, *outs)


def shifted(spread, taps, length):
    return [spread[:, taps - 1 - k : taps - 1 - k + length] for k in range(taps)]


def spread_sum(blocks):
    total = blocks[0].astype(F32)
    for b in blocks[1:]:
        total = total + b.astype(F32)
    return total


def reduce_xy(terms, x, y, z):
    rows, cols = terms.shape
    grp = rows // 16
    cut = (cols // 2 + 127) // 128 * 128
    view = terms.reshape(4, 4, grp, cols)

    def stage(part, axis_name, dim, mine, turned):
        size = part.shape[dim]

        def pick(step):
            at = (mine + step - (z if turned else 0) + 8) % size
            return lax.dynamic_index_in_dim(part, at, dim, keepdims=False)

        got = [pick(0)] + [rot(pick(j), axis_name, j) for j in (1, 2, 3)]
        return spread_sum(got)

    left = stage(view[..., :cut], "y", 1, y, False).astype(BF)
    left = stage(left, "x", 0, x, True)
    right = stage(view[..., cut:], "x", 0, x, True).astype(BF)
    right = stage(right, "y", 0, y, False)
    return jnp.concatenate([left, right], axis=1)


def weight_terms(acts, d_own, d_other, taps, length):
    acts_other = swap(acts)
    d_recv = swap(d_other)
    mine = jnp.concatenate(shifted(d_own, taps, length), axis=0)
    theirs = jnp.concatenate(shifted(d_recv, taps, length), axis=0)
    return (mm_cols(acts, mine) + mm_cols(acts_other, theirs)).astype(BF)


def block_back(spread, values_own, factor, sloped, weights, core):
    length = spread.shape[1] - 4
    own_w, other_w = weights
    taps, rows = own_w.shape[0], own_w.shape[1]
    width = own_w.shape[2]
    d_own = lax.dynamic_slice_in_dim(spread, core * rows, rows, 0)
    d_other = lax.dynamic_slice_in_dim(spread, (1 - core) * rows, rows, 0)
    part = None
    for weight, d in ((own_w, d_own), (other_w, d_other)):
        for k, piece in enumerate(shifted(d, taps, length)):
            term = mm_rows(weight[k], piece)
            part = term if part is None else part + term
    col = jnp.sum(part * sloped, axis=0, keepdims=True)
    high = col.astype(BF)
    low = (col - high.astype(F32)).astype(BF)
    tail = jnp.concatenate([high, low, jnp.zeros((14, length), BF)], axis=0)
    size = width // 4
    total = part[:size]
    for j in (1, 2, 3):
        sent = jnp.concatenate([part[j * size : (j + 1) * size].astype(BF), tail], axis=0)
        got = rot(sent, "z", j).astype(F32)
        total = total + got[:size]
        col = col + got[size : size + 1] + got[size + 1 : size + 2]
    values = values_own.astype(F32)
    _, slope = gelu_pair(values * factor)
    cubed = factor * factor * factor
    step = factor * (total * slope) - values * (cubed * col / width)
    return step, d_own, d_other


def on_device(features, weight_first, weight_widen, weight_second, weight_third, upstream):
    x, y, z, core = (lax.axis_index(a) for a in ("x", "y", "z", "core"))
    grad_scale = 1.0 / math.sqrt(features.shape[1] * 16)
    taps = weight_first.shape[0]

    feats = fine(features, core)
    ups = fine(upstream, core)
    long, short = feats.shape[1], ups.shape[1]
    gathered_a = gather_z(feats)
    up_spread = halo(ups)

    def both(weight):
        turned = turn(weight, z)
        return turned, swap(turned)

    w1, ww, w2, w3 = both(weight_first), both(weight_widen), both(weight_second), both(weight_third)

    factor_a, acts_a, sloped_a = activate(gathered_a)
    mixed_a = (feats.astype(F32) + conv(halo(acts_a), w1, long, core)).astype(BF)
    pair = (
        lax.broadcasted_iota(jnp.int32, (long, short), 0) // 2
        == lax.broadcasted_iota(jnp.int32, (long, short), 1)
    )
    pooled = mm(mixed_a, jnp.where(pair, 0.5, 0.0).astype(BF)).astype(BF)
    pooled_all = gather_z(pooled)
    widened = by_core(core, mm(ww[0], pooled_all), mm(ww[1], pooled_all)).astype(BF)
    gathered_b = gather_z(widened)
    factor_b, acts_b, sloped_b = activate(gathered_b)
    mixed_b = (widened.astype(F32) + conv(halo(acts_b), w2, short, core)).astype(BF)
    gathered_c = gather_z(mixed_b)
    factor_c, acts_c, sloped_c = activate(gathered_c)

    step, d_own, d_other = block_back(up_spread, mixed_b, factor_c, sloped_c, w3, core)
    terms_third = weight_terms(acts_c, d_own, d_other, taps, short)
    grad_mid = ups.astype(F32) + step
    mid_spread = halo(grad_mid.astype(BF))
    step, d_own, d_other = block_back(mid_spread, widened, factor_b, sloped_b, w2, core)
    terms_second = weight_terms(acts_b, d_own, d_other, taps, short)
    grad_top = grad_mid + step

    top_low = grad_top.astype(BF)
    rows = top_low.shape[0] // 2
    top_own = lax.dynamic_slice_in_dim(top_low, core * rows, rows, 0)
    top_other = lax.dynamic_slice_in_dim(top_low, (1 - core) * rows, rows, 0)
    part = mm_rows(ww[0], top_own) + mm_rows(ww[1], top_other)
    terms_widen = (
        mm_cols(pooled_all, top_own) + mm_cols(swap(pooled_all), swap(top_other))
    ).astype(BF)
    size = part.shape[0] // 4
    grad_pooled = part[:size]
    for j in (1, 2, 3):
        got = rot(part[j * size : (j + 1) * size].astype(BF), "z", j)
        grad_pooled = grad_pooled + got.astype(F32)
    grad_mixed = lax.dot_general(
        grad_pooled,
        jnp.where(pair, 0.5, 0.0).astype(F32),
        (((1,), (1,)), ((), ())),
        precision=lax.Precision.HIGHEST,
        preferred_element_type=F32,
    )
    mixed_spread = halo(grad_mixed.astype(BF))
    step, d_own, d_other = block_back(mixed_spread, feats, factor_a, sloped_a, w1, core)
    terms_first = weight_terms(acts_a, d_own, d_other, taps, long)
    grad_fine = (grad_mixed + step).astype(BF)

    rows = grad_fine.shape[0] // 2
    own = lax.dynamic_slice_in_dim(grad_fine, core * rows, rows, 0)
    other = lax.dynamic_slice_in_dim(grad_fine, (1 - core) * rows, rows, 0)
    grad_features = by_core(core, own, swap(other), axis=1)

    def taps_out(flat):
        grp = flat.shape[0]
        return (flat * grad_scale).reshape(grp, taps, -1).transpose(1, 0, 2)

    third = lax.psum_scatter(
        jnp.roll(terms_third, z * (terms_third.shape[0] // 4), axis=0),
        ("x", "y"),
        scatter_dimension=0,
        tiled=True,
    ).astype(F32)
    second = reduce_xy(terms_second, x, y, z)
    cut = terms_first.shape[1]
    last = reduce_xy(jnp.concatenate([terms_first, terms_widen], axis=1), x, y, z)
    return (
        grad_features,
        taps_out(last[:, :cut]),
        last[:, cut:] * grad_scale,
        taps_out(second),
        taps_out(third),
    )


def solution(mesh):
    axes = mesh.axis_names
    devices = mesh.devices
    if axes != ("seq", "chan"):
        devices = devices.T
    parts = Mesh(devices.reshape(4, 4, 4, 2), ("x", "y", "z", "core"))
    seq, chan = ("x", "y"), ("z", "core")
    placed = (
        P(chan, seq),
        P(None, chan, None),
        P(chan, None),
        P(None, chan, None),
        P(None, chan, None),
        P(chan, seq),
    )
    return jax.shard_map(
        on_device,
        mesh=parts,
        in_specs=placed,
        out_specs=(
            P(chan, seq),
            P(None, seq, chan),
            P(seq, chan),
            P(None, seq, chan),
            P(None, seq, chan),
        ),
        check_vma=False,
    )
```

```python
import math

import jax
import jax.numpy as jnp
from jax import lax
from jax.experimental import pallas as pl
from jax.experimental.pallas import tpu as pltpu
from jax.sharding import Mesh
from jax.sharding import PartitionSpec as P

EPSILON = 1e-06
ROOT_HALF = 0.7071067811865476
DENSITY_SCALE = 0.3989422804014327
BF = jnp.bfloat16
F32 = jnp.float32
SEQ = ("x", "y", "core")


def gelu_pair(s):
    half_erf = 0.5 * (1.0 + lax.erf(s * ROOT_HALF))
    return s * half_erf, half_erf + s * DENSITY_SCALE * jnp.exp(-0.5 * s * s)


def rot(block, axis, step):
    count = lax.axis_size(axis)
    return lax.ppermute(block, axis, [(i, (i + step) % count) for i in range(count)])


def swap(block):
    return lax.ppermute(block, "core", [(0, 1), (1, 0)])


def halo(block):
    count = math.prod(lax.axis_size(a) for a in SEQ)
    up = [(i, i + 1) for i in range(count - 1)]
    low = lax.ppermute(block[:, -2:], SEQ, up)
    high = lax.ppermute(block[:, :2], SEQ, [(b, a) for a, b in up])
    return jnp.concatenate([low, block, high], axis=1)


def mm(left, right):
    return jnp.dot(left, right, preferred_element_type=F32)


def mm_rows(left, right):
    return lax.dot_general(left, right, (((0,), (0,)), ((), ())), preferred_element_type=F32)


def by_core(core, own, other, axis=0):
    return jnp.where(
        core == 0,
        jnp.concatenate([own, other], axis=axis),
        jnp.concatenate([other, own], axis=axis),
    )


def fine(block, core):
    half = block.shape[1] // 2
    own = lax.dynamic_slice_in_dim(block, core * half, half, 1)
    other = lax.dynamic_slice_in_dim(block, (1 - core) * half, half, 1)
    return by_core(core, own, swap(other))


def gather_z(block, z):
    parts = [block] + [rot(block, "z", -j) for j in (1, 2, 3)]
    size = block.shape[0]
    twice = jnp.concatenate(parts + parts[:3], axis=0)
    return lax.dynamic_slice_in_dim(twice, ((4 - z) % 4) * size, 4 * size, 0)


def piece(part, z, j):
    size = part.shape[0] // 4
    return lax.dynamic_slice_in_dim(part, ((z + j) % 4) * size, size, 0)


def activate(gathered):
    values = gathered.astype(F32)
    factor = lax.rsqrt(jnp.mean(values * values, axis=0, keepdims=True) + EPSILON)
    act, slope = gelu_pair(values * factor)
    return factor, act.astype(BF), slope * values


def flat(weight):
    taps, rows, width = weight.shape
    return weight.reshape(taps * rows, width)


def conv(padded, weights, taps, length, core):
    outs = []
    for weight in weights:
        rows = weight.shape[0] // taps
        wide = mm(weight, padded)
        total = wide[:rows, :length]
        for k in range(1, taps):
            total = total + wide[k * rows : (k + 1) * rows, k : k + length]
        outs.append(total)
    return by_core(core, *outs)


def shifted(spread, taps, length):
    return jnp.concatenate(
        [spread[:, taps - 1 - k : taps - 1 - k + length] for k in range(taps)], axis=0
    )


def spread_sum(blocks):
    total = blocks[0].astype(F32)
    for b in blocks[1:]:
        total = total + b.astype(F32)
    return total


def terms_kernel(y_ref, a_ref, b_ref, p_ref, q_ref, o0, o1, o2, o3, scratch):
    group = o0.shape[1]
    dims = (((1,), (1,)), ((), ()))
    scratch[...] = lax.dot_general(
        a_ref[...], p_ref[...], dims, preferred_element_type=F32
    ) + lax.dot_general(b_ref[...], q_ref[...], dims, preferred_element_type=F32)
    for j, out in enumerate((o0, o1, o2, o3)):
        at = pl.multiple_of(lax.rem(y_ref[0] + j, 4) * group, 16)
        out[0] = scratch[pl.ds(at, group), :].astype(BF)


def weight_terms(acts, acts_other, mine, theirs, y):
    width, length = acts.shape
    cols = mine.shape[0]
    rows, group = width // 4, width // 16
    row_spec = pl.BlockSpec((rows, length), lambda i, y: (i, 0))
    col_spec = pl.BlockSpec((cols, length), lambda i, y: (0, 0))
    out_spec = pl.BlockSpec((1, group, cols), lambda i, y: (i, 0, 0))
    return pl.pallas_call(
        terms_kernel,
        grid_spec=pltpu.PrefetchScalarGridSpec(
            num_scalar_prefetch=1,
            grid=(4,),
            in_specs=[row_spec, row_spec, col_spec, col_spec],
            out_specs=[out_spec] * 4,
            scratch_shapes=[pltpu.VMEM((rows, cols), F32)],
        ),
        out_shape=[jax.ShapeDtypeStruct((4, group, cols), BF)] * 4,
        cost_estimate=pl.CostEstimate(
            flops=4 * width * cols * length,
            bytes_accessed=4 * (width + cols) * length + 2 * width * cols,
            transcendentals=0,
        ),
    )(y.reshape(1).astype(jnp.int32), acts, acts_other, mine, theirs)


def reduce_y(terms):
    return spread_sum([terms[0]] + [rot(terms[j], "y", j) for j in (1, 2, 3)]).astype(BF)


def reduce_x(terms, x):
    def pick(j):
        return lax.dynamic_index_in_dim(terms, (x + j) % 4, 0, keepdims=False)

    return spread_sum([pick(0)] + [rot(pick(j), "x", j) for j in (1, 2, 3)])


def halves(block, core):
    rows = block.shape[0] // 2
    own = lax.dynamic_slice_in_dim(block, core * rows, rows, 0)
    other = lax.dynamic_slice_in_dim(block, (1 - core) * rows, rows, 0)
    return own, other


def block_back(spread, values_own, factor, sloped, weights, taps, z, core):
    length = spread.shape[1] - 4
    own_w, other_w = weights
    width = own_w.shape[1]
    d_own, d_other = halves(spread, core)
    d_own, d_other = shifted(d_own, taps, length), shifted(d_other, taps, length)
    d_recv = swap(d_other)
    part = mm_rows(own_w, d_own) + mm_rows(other_w, d_other)
    col = jnp.sum(part * sloped, axis=0, keepdims=True)
    high = col.astype(BF)
    low = (col - high.astype(F32)).astype(BF)
    tail = jnp.concatenate([high, low, jnp.zeros((14, length), BF)], axis=0)
    size = width // 4
    got = [
        rot(jnp.concatenate([piece(part, z, j).astype(BF), tail], axis=0), "z", j)
        for j in (1, 2, 3)
    ]

    def finish(got):
        total = piece(part, z, 0)
        sums = col
        for g in got:
            g = g.astype(F32)
            total = total + g[:size]
            sums = sums + g[size : size + 1] + g[size + 1 : size + 2]
        values = values_own.astype(F32)
        _, slope = gelu_pair(values * factor)
        cubed = factor * factor * factor
        return factor * (total * slope) - values * (cubed * sums / width)

    return got, finish, d_own, d_recv


def on_device(features, weight_first, weight_widen, weight_second, weight_third, upstream):
    x, y, z, core = (lax.axis_index(a) for a in ("x", "y", "z", "core"))
    grad_scale = 1.0 / math.sqrt(features.shape[1] * 16)
    taps = weight_first.shape[0]
    tie = lax.optimization_barrier

    feats = fine(features, core)
    ups = fine(upstream, core)
    long, short = feats.shape[1], ups.shape[1]
    gathered_a = gather_z(feats, z)
    up_spread = halo(ups)

    def both(weight):
        return weight, swap(weight)

    w1, ww, w2, w3 = (
        both(flat(weight_first)),
        both(weight_widen),
        both(flat(weight_second)),
        both(flat(weight_third)),
    )

    factor_a, acts_a, sloped_a = activate(gathered_a)
    mixed_a = (feats.astype(F32) + conv(halo(acts_a), w1, taps, long, core)).astype(BF)
    acts_a_other = swap(acts_a)
    pair = (
        lax.broadcasted_iota(jnp.int32, (long, short), 0) // 2
        == lax.broadcasted_iota(jnp.int32, (long, short), 1)
    )
    pooled = mm(mixed_a, jnp.where(pair, 0.5, 0.0).astype(BF)).astype(BF)
    pooled_all = gather_z(pooled, z)
    pooled_other = swap(pooled_all)
    widened = by_core(core, mm(ww[0], pooled_all), mm(ww[1], pooled_all)).astype(BF)
    gathered_b = gather_z(widened, z)
    factor_b, acts_b, sloped_b = activate(gathered_b)
    mixed_b = (widened.astype(F32) + conv(halo(acts_b), w2, taps, short, core)).astype(BF)
    acts_b_other = swap(acts_b)
    gathered_c = gather_z(mixed_b, z)
    factor_c, acts_c, sloped_c = activate(gathered_c)
    acts_c_other = swap(acts_c)

    got, finish, mine, theirs = block_back(
        up_spread, mixed_b, factor_c, sloped_c, w3, taps, z, core
    )
    third = weight_terms(acts_c, acts_c_other, mine, theirs, y)
    got, third = tie((got, third))
    grad_mid = ups.astype(F32) + finish(got)
    got, finish, mine, theirs = block_back(
        halo(grad_mid.astype(BF)), widened, factor_b, sloped_b, w2, taps, z, core
    )
    second = weight_terms(acts_b, acts_b_other, mine, theirs, y)
    got, second = tie((got, second))
    grad_top = grad_mid + finish(got)

    top_own, top_other = halves(grad_top.astype(BF), core)
    part = mm_rows(ww[0], top_own) + mm_rows(ww[1], top_other)
    got = [rot(piece(part, z, j).astype(BF), "z", j) for j in (1, 2, 3)]
    widen = weight_terms(pooled_all, pooled_other, top_own, swap(top_other), y)
    third = reduce_y(third)
    got, widen, third = tie((got, widen, third))
    grad_pooled = piece(part, z, 0)
    for g in got:
        grad_pooled = grad_pooled + g.astype(F32)
    grad_mixed = lax.dot_general(
        grad_pooled,
        jnp.where(pair, 0.5, 0.0).astype(F32),
        (((1,), (1,)), ((), ())),
        precision=lax.Precision.HIGHEST,
        preferred_element_type=F32,
    )
    got, finish, mine, theirs = block_back(
        halo(grad_mixed.astype(BF)), feats, factor_a, sloped_a, w1, taps, z, core
    )
    first = weight_terms(acts_a, acts_a_other, mine, theirs, y)
    got, first = tie((got, first))
    grad_fine = (grad_mixed + finish(got)).astype(BF)

    own, other = halves(grad_fine, core)
    grad_features = by_core(core, own, swap(other), axis=1)

    def taps_out(flat_sum):
        grp = flat_sum.shape[0]
        return (flat_sum * grad_scale).reshape(grp, taps, -1).transpose(1, 0, 2)

    third = reduce_x(third, x)
    second = reduce_x(reduce_y(second), x)
    cut = first[0].shape[2]
    last = [jnp.concatenate(pair_of, axis=2) for pair_of in zip(first, widen)]
    last = reduce_x(reduce_y(last), x)
    return (
        grad_features,
        taps_out(last[:, :cut]),
        last[:, cut:] * grad_scale,
        taps_out(second),
        taps_out(third),
    )


def solution(mesh):
    axes = mesh.axis_names
    devices = mesh.devices
    if axes != ("seq", "chan"):
        devices = devices.T
    parts = Mesh(devices.reshape(4, 4, 4, 2), ("x", "y", "z", "core"))
    seq, chan = ("x", "y"), ("z", "core")
    placed = (
        P(chan, seq),
        P(None, chan, None),
        P(chan, None),
        P(None, chan, None),
        P(None, chan, None),
        P(chan, seq),
    )
    return jax.shard_map(
        on_device,
        mesh=parts,
        in_specs=placed,
        out_specs=(
            P(chan, seq),
            P(None, seq, chan),
            P(seq, chan),
            P(None, seq, chan),
            P(None, seq, chan),
        ),
        check_vma=False,
    )
```

```python
import functools
import math

import jax
import jax.numpy as jnp
from jax import lax
from jax.experimental import pallas as pl
from jax.experimental.pallas import tpu as pltpu
from jax.sharding import Mesh
from jax.sharding import PartitionSpec as P

EPSILON = 1e-06
ROOT_HALF = 0.7071067811865476
DENSITY_SCALE = 0.3989422804014327
BF = jnp.bfloat16
F32 = jnp.float32
SEQ = ("x", "y", "core")


def gelu_pair(s):
    half_erf = 0.5 * (1.0 + lax.erf(s * ROOT_HALF))
    return s * half_erf, half_erf + s * DENSITY_SCALE * jnp.exp(-0.5 * s * s)


def rot(block, axis, step):
    count = lax.axis_size(axis)
    return lax.ppermute(block, axis, [(i, (i + step) % count) for i in range(count)])


def swap(block):
    return lax.ppermute(block, "core", [(0, 1), (1, 0)])


def halo(block):
    count = math.prod(lax.axis_size(a) for a in SEQ)
    up = [(i, i + 1) for i in range(count - 1)]
    low = lax.ppermute(block[:, -2:], SEQ, up)
    high = lax.ppermute(block[:, :2], SEQ, [(b, a) for a, b in up])
    return jnp.concatenate([low, block, high], axis=1)


def mm(left, right):
    return jnp.dot(left, right, preferred_element_type=F32)


def mm_rows(left, right):
    return lax.dot_general(left, right, (((0,), (0,)), ((), ())), preferred_element_type=F32)


def by_core(core, own, other, axis=0):
    return jnp.where(
        core == 0,
        jnp.concatenate([own, other], axis=axis),
        jnp.concatenate([other, own], axis=axis),
    )


def fine(block, core):
    half = block.shape[1] // 2
    own = lax.dynamic_slice_in_dim(block, core * half, half, 1)
    other = lax.dynamic_slice_in_dim(block, (1 - core) * half, half, 1)
    return by_core(core, own, swap(other))


def gather_z(block, z):
    parts = [block] + [rot(block, "z", -j) for j in (1, 2, 3)]
    size = block.shape[0]
    twice = jnp.concatenate(parts + parts[:3], axis=0)
    return lax.dynamic_slice_in_dim(twice, ((4 - z) % 4) * size, 4 * size, 0)


def piece(part, z, j):
    size = part.shape[0] // 4
    return lax.dynamic_slice_in_dim(part, ((z + j) % 4) * size, size, 0)


def activate(gathered):
    values = gathered.astype(F32)
    factor = lax.rsqrt(jnp.mean(values * values, axis=0, keepdims=True) + EPSILON)
    act, slope = gelu_pair(values * factor)
    return factor, act.astype(BF), slope * values


def flat(weight):
    taps, rows, width = weight.shape
    return weight.reshape(taps * rows, width)


def conv(padded, weights, taps, length, core):
    outs = []
    for weight in weights:
        rows = weight.shape[0] // taps
        wide = mm(weight, padded)
        total = wide[:rows, :length]
        for k in range(1, taps):
            total = total + wide[k * rows : (k + 1) * rows, k : k + length]
        outs.append(total)
    return by_core(core, *outs)


def shift_kernel(core_ref, spread_ref, own_ref, other_ref):
    rows, length = own_ref.shape[1:]
    for ref, at in ((own_ref, core_ref[0] * rows), (other_ref, (1 - core_ref[0]) * rows)):
        block = spread_ref[pl.ds(pl.multiple_of(at, 16), rows), :].astype(F32)
        for k in range(ref.shape[0]):
            start = ref.shape[0] - 1 - k
            ref[k] = block[:, start : start + length].astype(BF)


def shifted(spread, core, taps):
    rows, length = spread.shape[0] // 2, spread.shape[1] - taps + 1
    own, other = pl.pallas_call(
        shift_kernel,
        in_specs=[pl.BlockSpec(memory_space=pltpu.SMEM), pl.BlockSpec(memory_space=pltpu.VMEM)],
        out_specs=[pl.BlockSpec(memory_space=pltpu.VMEM)] * 2,
        out_shape=[jax.ShapeDtypeStruct((taps, rows, length), BF)] * 2,
        cost_estimate=pl.CostEstimate(
            flops=0, bytes_accessed=4 * (taps + 1) * rows * length, transcendentals=0
        ),
    )(core.reshape(1).astype(jnp.int32), spread)
    return own.reshape(taps * rows, length), other.reshape(taps * rows, length)


def spread_sum(blocks):
    total = blocks[0].astype(F32)
    for b in blocks[1:]:
        total = total + b.astype(F32)
    return total


def terms_kernel(at_ref, *refs, products, cuts):
    ins, outs, scratch = refs[: 4 * products], refs[4 * products : -1], refs[-1]
    left, right = outs[:4], outs[4:]
    group = scratch.shape[0] // 4
    dims = (((1,), (1,)), ((), ()))
    start = 0
    for p in range(products):
        a, b, d, e = ins[4 * p : 4 * p + 4]
        total = lax.dot_general(a[...], d[...], dims, preferred_element_type=F32)
        total = total + lax.dot_general(b[...], e[...], dims, preferred_element_type=F32)
        end = start + d.shape[0]
        scratch[:, start:end] = total
        start = min(cuts[p], scratch.shape[1])
        if start > end:
            scratch[:, end:start] = jnp.zeros((scratch.shape[0], start - end), F32)
    for j in range(4):
        rows = pl.ds(pl.multiple_of(lax.rem(at_ref[1] + j, 4) * group, 16), group)
        block = scratch[rows, :].astype(BF)
        width = left[j].shape[2]
        left[j][0] = block[:, :width]
        for i, out in enumerate(right):

            @pl.when(pl.program_id(0) == i)
            def _():
                out[j] = block[:, width:]


def weight_terms(products, x, y, split):
    width, length = products[0][0].shape
    rows, group = width // 4, width // 16
    cuts, total = [], 0
    specs, args, flops = [], [], 0
    for acts, acts_other, mine, theirs in products:
        cols, span = mine.shape
        row_spec = pl.BlockSpec((rows, span), lambda i, at: (lax.rem(at[0] + i, 4), 0))
        col_spec = pl.BlockSpec((cols, span), lambda i, at: (0, 0))
        specs += [row_spec, row_spec, col_spec, col_spec]
        args += [acts, acts_other, mine, theirs]
        flops += 4 * width * cols * span
        end = total + cols
        total = (end + 127) // 128 * 128
        cuts.append(total)
    left, right = (end, 0) if split is None else (split, end - split)
    out_specs = [pl.BlockSpec((1, group, left), lambda i, at: (i, 0, 0))] * 4
    out_shape = [jax.ShapeDtypeStruct((4, group, left), BF)] * 4
    if right:
        out_specs += [pl.BlockSpec((4, group, right), lambda i, at: (0, 0, 0))] * 4
        out_shape += [jax.ShapeDtypeStruct((4, group, right), BF)] * 4
    outs = pl.pallas_call(
        functools.partial(terms_kernel, products=len(products), cuts=cuts),
        grid_spec=pltpu.PrefetchScalarGridSpec(
            num_scalar_prefetch=1,
            grid=(4,),
            in_specs=specs,
            out_specs=out_specs,
            scratch_shapes=[pltpu.VMEM((rows, end), F32)],
        ),
        out_shape=out_shape,
        cost_estimate=pl.CostEstimate(
            flops=flops, bytes_accessed=4 * width * length + 2 * width * end, transcendentals=0
        ),
    )(jnp.stack([x, y]).astype(jnp.int32), *args)
    return list(outs)


def scatter(blocks, axis):
    return spread_sum([blocks[0]] + [rot(blocks[j], axis, j) for j in (1, 2, 3)])


def reduce_first(terms):
    out = [scatter(terms[:4], "y").astype(BF)]
    if len(terms) > 4:
        out.append(scatter(terms[4:], "x").astype(BF))
    return out


def reduce_last(sums):
    return jnp.concatenate([scatter(s, axis) for s, axis in zip(sums, ("x", "y"))], axis=1)


def halves(block, core):
    rows = block.shape[0] // 2
    own = lax.dynamic_slice_in_dim(block, core * rows, rows, 0)
    other = lax.dynamic_slice_in_dim(block, (1 - core) * rows, rows, 0)
    return own, other


def block_back(d_own, d_other, values_own, factor, sloped, weights, z):
    own_w, other_w = weights
    length = d_own.shape[1]
    width = own_w.shape[1]
    part = mm_rows(own_w, d_own) + mm_rows(other_w, d_other)
    col = jnp.sum(part * sloped, axis=0, keepdims=True)
    high = col.astype(BF)
    low = (col - high.astype(F32)).astype(BF)
    tail = jnp.concatenate([high, low, jnp.zeros((14, length), BF)], axis=0)
    size = width // 4
    got = [
        rot(jnp.concatenate([piece(part, z, j).astype(BF), tail], axis=0), "z", j)
        for j in (1, 2, 3)
    ]

    def finish(got):
        total = piece(part, z, 0)
        sums = col
        for g in got:
            total = total + g[:size].astype(F32)
            sums = sums + g[size : size + 1].astype(F32) + g[size + 1 : size + 2].astype(F32)
        values = values_own.astype(F32)
        _, slope = gelu_pair(values * factor)
        cubed = factor * factor * factor
        return factor * (total * slope) - values * (cubed * sums / width)

    return got, finish


def on_device(features, weight_first, weight_widen, weight_second, weight_third, upstream):
    x, y, z, core = (lax.axis_index(a) for a in ("x", "y", "z", "core"))
    grad_scale = 1.0 / math.sqrt(features.shape[1] * 16)
    taps = weight_first.shape[0]
    tie = lax.optimization_barrier

    feats = fine(features, core)
    feats, upstream, weight_first, weight_widen = tie(
        (feats, upstream, weight_first, weight_widen)
    )
    long, short = feats.shape[1], upstream.shape[1] // 2
    gathered_a = gather_z(feats, z)

    def both(weight):
        return weight, swap(weight)

    w1, ww = both(flat(weight_first)), both(weight_widen)
    ups = fine(upstream, core)
    w1, ww, ups, weight_second, weight_third = tie((w1, ww, ups, weight_second, weight_third))
    w2, w3 = both(flat(weight_second)), both(flat(weight_third))

    factor_a, acts_a, sloped_a = activate(gathered_a)
    mixed_a = (feats.astype(F32) + conv(halo(acts_a), w1, taps, long, core)).astype(BF)
    acts_a_other = swap(acts_a)
    pair = (
        lax.broadcasted_iota(jnp.int32, (long, short), 0) // 2
        == lax.broadcasted_iota(jnp.int32, (long, short), 1)
    )
    pooled = mm(mixed_a, jnp.where(pair, 0.5, 0.0).astype(BF)).astype(BF)
    pooled, ups = tie((pooled, ups))
    pooled_all = gather_z(pooled, z)
    up_own, up_other = shifted(halo(ups), core, taps)
    pooled_all, acts_a_other, up_own, up_other = tie((pooled_all, acts_a_other, up_own, up_other))
    pooled_other = swap(pooled_all)
    up_recv = swap(up_other)
    widened = by_core(core, mm(ww[0], pooled_all), mm(ww[1], pooled_all)).astype(BF)
    gathered_b, pooled_other, up_recv = tie((gather_z(widened, z), pooled_other, up_recv))
    factor_b, acts_b, sloped_b = activate(gathered_b)
    mixed_b = (widened.astype(F32) + conv(halo(acts_b), w2, taps, short, core)).astype(BF)
    gathered_c, acts_b_other = tie((gather_z(mixed_b, z), swap(acts_b)))
    factor_c, acts_c, sloped_c = activate(gathered_c)
    acts_c_other = swap(acts_c)

    got, finish = block_back(up_own, up_other, mixed_b, factor_c, sloped_c, w3, z)
    third = weight_terms([(acts_c, acts_c_other, up_own, up_recv)], x, y, None)
    got, third = tie((got, third))
    grad_mid = ups.astype(F32) + finish(got)
    mid_spread, third = tie((halo(grad_mid.astype(BF)), third))
    d_own, d_other = shifted(mid_spread, core, taps)
    third = reduce_first(third)
    got, finish = block_back(d_own, d_other, widened, factor_b, sloped_b, w2, z)
    cut = w2[0].shape[0] // 2 // 128 * 128 + 128
    second = weight_terms([(acts_b, acts_b_other, d_own, swap(d_other))], x, y, cut)
    got, second = tie((got, second))
    grad_top = grad_mid + finish(got)

    top_own, top_other = halves(grad_top.astype(BF), core)
    part = mm_rows(ww[0], top_own) + mm_rows(ww[1], top_other)
    got = [rot(piece(part, z, j).astype(BF), "z", j) for j in (1, 2, 3)]
    got, top_recv = tie((got, swap(top_other)))
    grad_pooled = piece(part, z, 0)
    for g in got:
        grad_pooled = grad_pooled + g.astype(F32)
    grad_mixed = lax.dot_general(
        grad_pooled,
        jnp.where(pair, 0.5, 0.0).astype(F32),
        (((1,), (1,)), ((), ())),
        precision=lax.Precision.HIGHEST,
        preferred_element_type=F32,
    )
    mixed_spread, second, third = tie((halo(grad_mixed.astype(BF)), second, third))
    d_own, d_other = shifted(mixed_spread, core, taps)
    second = reduce_first(second)
    third = reduce_last(third)
    got, finish = block_back(d_own, d_other, feats, factor_a, sloped_a, w1, z)
    first = weight_terms(
        [
            (acts_a, acts_a_other, d_own, swap(d_other)),
            (pooled_all, pooled_other, top_own, top_recv),
        ],
        x,
        y,
        384,
    )
    got, first = tie((got, first))
    grad_fine = (grad_mixed + finish(got)).astype(BF)

    own, other = halves(grad_fine, core)
    grad_features = by_core(core, own, swap(other), axis=1)

    def taps_out(flat_sum):
        grp = flat_sum.shape[0]
        return (flat_sum * grad_scale).reshape(grp, taps, -1).transpose(1, 0, 2)

    last = reduce_last(reduce_first(first))
    cut = w1[0].shape[0]
    return (
        grad_features,
        taps_out(last[:, :cut]),
        last[:, -weight_widen.shape[0] :] * grad_scale,
        taps_out(reduce_last(second)),
        taps_out(third),
    )


def solution(mesh):
    axes = mesh.axis_names
    devices = mesh.devices
    if axes != ("seq", "chan"):
        devices = devices.T
    parts = Mesh(devices.reshape(4, 4, 4, 2), ("x", "y", "z", "core"))
    seq, chan = ("x", "y"), ("z", "core")
    placed = (
        P(chan, seq),
        P(None, chan, None),
        P(chan, None),
        P(None, chan, None),
        P(None, chan, None),
        P(chan, seq),
    )
    return jax.shard_map(
        on_device,
        mesh=parts,
        in_specs=placed,
        out_specs=(
            P(chan, seq),
            P(None, seq, chan),
            P(seq, chan),
            P(None, seq, chan),
            P(None, seq, chan),
        ),
        check_vma=False,
    )
```

```python
import functools
import math

import jax
import jax.numpy as jnp
from jax import lax
from jax.experimental import pallas as pl
from jax.experimental.pallas import tpu as pltpu
from jax.sharding import Mesh
from jax.sharding import PartitionSpec as P

EPSILON = 1e-06
ROOT_HALF = 0.7071067811865476
DENSITY_SCALE = 0.3989422804014327
BF = jnp.bfloat16
F32 = jnp.float32
SEQ = ("x", "y", "core")


def gelu_pair(s):
    half_erf = 0.5 * (1.0 + lax.erf(s * ROOT_HALF))
    return s * half_erf, half_erf + s * DENSITY_SCALE * jnp.exp(-0.5 * s * s)


def rot(block, axis, step):
    return lax.ppermute(block, axis, [(i, i ^ step) for i in range(lax.axis_size(axis))])


def swap(block):
    return lax.ppermute(block, "core", [(0, 1), (1, 0)])


def halo(block, core):
    count = math.prod(lax.axis_size(a) for a in SEQ)
    pairs = [(i, i + 1) for i in range(1, count - 1, 2)]
    first = core == 0
    head, last = block[:, :2], block[:, -2:]
    far = lax.ppermute(jnp.where(first, head, last), SEQ, pairs + [(b, a) for a, b in pairs])
    near = swap(jnp.where(first, last, head))
    return jnp.concatenate([jnp.where(first, far, near), block, jnp.where(first, near, far)], axis=1)


def mm(left, right):
    return jnp.dot(left, right, preferred_element_type=F32)


def mm_rows(left, right):
    return lax.dot_general(left, right, (((0,), (0,)), ((), ())), preferred_element_type=F32)


def by_core(core, own, other, axis=0):
    return jnp.where(
        core == 0,
        jnp.concatenate([own, other], axis=axis),
        jnp.concatenate([other, own], axis=axis),
    )


def fine(block, core):
    half = block.shape[1] // 2
    own = lax.dynamic_slice_in_dim(block, core * half, half, 1)
    other = lax.dynamic_slice_in_dim(block, (1 - core) * half, half, 1)
    return by_core(core, own, swap(other))


def exchange(block):
    return [block] + [rot(block, "z", j) for j in (1, 2, 3)]


def place_kernel(z_ref, *refs):
    ins, out = refs[:4], refs[4]
    size = ins[0].shape[0]
    for j, ref in enumerate(ins):
        out[pl.ds(pl.multiple_of((z_ref[0] ^ j) * size, 16), size), :] = ref[...]


def in_vmem(kernel, scalar, args, out_shape, flops, transcendentals=0):
    vmem = pl.BlockSpec(memory_space=pltpu.VMEM)
    size = sum(a.size * a.dtype.itemsize for a in args) + sum(
        o.size * o.dtype.itemsize for o in out_shape
    )
    return pl.pallas_call(
        kernel,
        in_specs=[pl.BlockSpec(memory_space=pltpu.SMEM)] + [vmem] * len(args),
        out_specs=[vmem] * len(out_shape),
        out_shape=out_shape,
        cost_estimate=pl.CostEstimate(
            flops=flops, bytes_accessed=size, transcendentals=transcendentals
        ),
    )(scalar.reshape(1).astype(jnp.int32), *args)


def place(blocks, z):
    size, length = blocks[0].shape
    return in_vmem(
        place_kernel, z, blocks, [jax.ShapeDtypeStruct((4 * size, length), BF)], 0
    )[0]


def piece(part, z, j):
    size = part.shape[0] // 4
    return lax.dynamic_slice_in_dim(part, (z ^ j) * size, size, 0)


def act_kernel(z_ref, *refs):
    ins, (factor_ref, act_ref, sloped_ref) = refs[:4], refs[4:]
    size, length = ins[0].shape
    step = 32

    def squares(i, total):
        for ref in ins:
            v = ref[pl.ds(pl.multiple_of(i * step, step), step), :].astype(F32)
            total = total + v * v
        return total

    total = lax.fori_loop(0, size // step, squares, jnp.zeros((step, length), F32))
    mean = jnp.sum(total, axis=0, keepdims=True) * (1.0 / (4 * size))
    factor = lax.rsqrt(mean + EPSILON)
    factor_ref[...] = factor
    for j, ref in enumerate(ins):
        start = (z_ref[0] ^ j) * size

        @pl.loop(0, size // step)
        def _(i):
            v = ref[pl.ds(pl.multiple_of(i * step, step), step), :].astype(F32)
            act, slope = gelu_pair(v * factor)
            at = pl.ds(pl.multiple_of(start + i * step, step), step)
            act_ref[at, :] = act.astype(BF)
            sloped_ref[at, :] = slope * v


def activate(blocks, z):
    size, length = blocks[0].shape
    full = (4 * size, length)
    return in_vmem(
        act_kernel,
        z,
        blocks,
        [
            jax.ShapeDtypeStruct((1, length), F32),
            jax.ShapeDtypeStruct(full, BF),
            jax.ShapeDtypeStruct(full, F32),
        ],
        80 * size * length,
        8 * size * length,
    )


def flat(weight):
    taps, rows, width = weight.shape
    return weight.reshape(taps * rows, width)


def conv(padded, weights, taps, length, core):
    outs = []
    for weight in weights:
        rows = weight.shape[0] // taps
        wide = mm(weight, padded)
        total = wide[:rows, :length]
        for k in range(1, taps):
            total = total + wide[k * rows : (k + 1) * rows, k : k + length]
        outs.append(total)
    return by_core(core, *outs)


def shift_kernel(core_ref, spread_ref, own_ref, other_ref):
    rows, length = own_ref.shape[1:]
    for ref, at in ((own_ref, core_ref[0] * rows), (other_ref, (1 - core_ref[0]) * rows)):
        block = spread_ref[pl.ds(pl.multiple_of(at, 16), rows), :].astype(F32)
        for k in range(ref.shape[0]):
            start = ref.shape[0] - 1 - k
            ref[k] = block[:, start : start + length].astype(BF)


def shifted(spread, core, taps):
    rows, length = spread.shape[0] // 2, spread.shape[1] - taps + 1
    own, other = pl.pallas_call(
        shift_kernel,
        in_specs=[pl.BlockSpec(memory_space=pltpu.SMEM), pl.BlockSpec(memory_space=pltpu.VMEM)],
        out_specs=[pl.BlockSpec(memory_space=pltpu.VMEM)] * 2,
        out_shape=[jax.ShapeDtypeStruct((taps, rows, length), BF)] * 2,
        cost_estimate=pl.CostEstimate(
            flops=0, bytes_accessed=4 * (taps + 1) * rows * length, transcendentals=0
        ),
    )(core.reshape(1).astype(jnp.int32), spread)
    return own.reshape(taps * rows, length), other.reshape(taps * rows, length)


def spread_sum(blocks):
    total = blocks[0].astype(F32)
    for b in blocks[1:]:
        total = total + b.astype(F32)
    return total


def terms_kernel(at_ref, *refs, products, cuts):
    ins, outs, scratch = refs[: 4 * products], refs[4 * products : -1], refs[-1]
    left, right = outs[:4], outs[4:]
    group = scratch.shape[0] // 4
    dims = (((1,), (1,)), ((), ()))
    start = 0
    for p in range(products):
        a, b, d, e = ins[4 * p : 4 * p + 4]
        total = lax.dot_general(a[...], d[...], dims, preferred_element_type=F32)
        total = total + lax.dot_general(b[...], e[...], dims, preferred_element_type=F32)
        end = start + d.shape[0]
        scratch[:, start:end] = total
        start = min(cuts[p], scratch.shape[1])
        if start > end:
            scratch[:, end:start] = jnp.zeros((scratch.shape[0], start - end), F32)
    for j in range(4):
        rows = pl.ds(pl.multiple_of((at_ref[1] ^ j) * group, 16), group)
        block = scratch[rows, :].astype(BF)
        width = left[j].shape[2]
        left[j][0] = block[:, :width]
        for i, out in enumerate(right):

            @pl.when(pl.program_id(0) == i)
            def _():
                out[j] = block[:, width:]


def weight_terms(products, x, y, split):
    width, length = products[0][0].shape
    rows, group = width // 4, width // 16
    cuts, total = [], 0
    specs, args, flops = [], [], 0
    for acts, acts_other, mine, theirs in products:
        cols, span = mine.shape
        row_spec = pl.BlockSpec((rows, span), lambda i, at: (at[0] ^ i, 0))
        col_spec = pl.BlockSpec((cols, span), lambda i, at: (0, 0))
        specs += [row_spec, row_spec, col_spec, col_spec]
        args += [acts, acts_other, mine, theirs]
        flops += 4 * width * cols * span
        end = total + cols
        total = (end + 127) // 128 * 128
        cuts.append(total)
    left, right = (end, 0) if split is None else (split, end - split)
    out_specs = [pl.BlockSpec((1, group, left), lambda i, at: (i, 0, 0))] * 4
    out_shape = [jax.ShapeDtypeStruct((4, group, left), BF)] * 4
    if right:
        out_specs += [pl.BlockSpec((4, group, right), lambda i, at: (0, 0, 0))] * 4
        out_shape += [jax.ShapeDtypeStruct((4, group, right), BF)] * 4
    outs = pl.pallas_call(
        functools.partial(terms_kernel, products=len(products), cuts=cuts),
        grid_spec=pltpu.PrefetchScalarGridSpec(
            num_scalar_prefetch=1,
            grid=(4,),
            in_specs=specs,
            out_specs=out_specs,
            scratch_shapes=[pltpu.VMEM((rows, end), F32)],
        ),
        out_shape=out_shape,
        cost_estimate=pl.CostEstimate(
            flops=flops, bytes_accessed=4 * width * length + 2 * width * end, transcendentals=0
        ),
    )(jnp.stack([x, y]).astype(jnp.int32), *args)
    return list(outs)


def send(blocks, axis):
    return [blocks[0]] + [rot(blocks[j], axis, j) for j in (1, 2, 3)]


def send_first(terms):
    out = [send(terms[:4], "y")]
    if len(terms) > 4:
        out.append(send(terms[4:], "x"))
    return out


def reduce_last(got):
    out = []
    for blocks, axis in zip(got, ("x", "y")):
        out.append(spread_sum(send(spread_sum(blocks).astype(BF), axis)))
    return jnp.concatenate(out, axis=1)


def send_z(sent):
    return [rot(m, "z", j + 1) for j, m in enumerate(sent)]


def halves(block, core):
    rows = block.shape[0] // 2
    own = lax.dynamic_slice_in_dim(block, core * rows, rows, 0)
    other = lax.dynamic_slice_in_dim(block, (1 - core) * rows, rows, 0)
    return own, other


def block_back(d_own, d_other, values_own, factor, sloped, weights, z):
    own_w, other_w = weights
    length = d_own.shape[1]
    width = own_w.shape[1]
    part = mm_rows(own_w, d_own) + mm_rows(other_w, d_other)
    col = jnp.sum(part * sloped, axis=0, keepdims=True)
    high = col.astype(BF)
    low = (col - high.astype(F32)).astype(BF)
    tail = jnp.concatenate([high, low, jnp.zeros((14, length), BF)], axis=0)
    size = width // 4
    sent = [jnp.concatenate([piece(part, z, j).astype(BF), tail], axis=0) for j in (1, 2, 3)]

    def finish(got):
        total = piece(part, z, 0)
        sums = col
        for g in got:
            total = total + g[:size].astype(F32)
            sums = sums + g[size : size + 1].astype(F32) + g[size + 1 : size + 2].astype(F32)
        values = values_own.astype(F32)
        _, slope = gelu_pair(values * factor)
        cubed = factor * factor * factor
        return factor * (total * slope) - values * (cubed * sums / width)

    return sent, finish


def on_device(features, weight_first, weight_widen, weight_second, weight_third, upstream):
    x, y, z, core = (lax.axis_index(a) for a in ("x", "y", "z", "core"))
    grad_scale = 1.0 / math.sqrt(features.shape[1] * 16)
    taps = weight_first.shape[0]
    tie = lax.optimization_barrier

    feats = fine(features, core)
    feats, upstream, weight_first, weight_widen = tie(
        (feats, upstream, weight_first, weight_widen)
    )
    long, short = feats.shape[1], upstream.shape[1] // 2
    blocks_a = exchange(feats)

    def both(weight):
        return weight, swap(weight)

    w1, ww = both(flat(weight_first)), both(weight_widen)
    ups = fine(upstream, core)
    w1, ww, ups, weight_second, weight_third = tie((w1, ww, ups, weight_second, weight_third))
    w2, w3 = both(flat(weight_second)), both(flat(weight_third))

    factor_a, acts_a, sloped_a = activate(blocks_a, z)
    mixed_a = (feats.astype(F32) + conv(halo(acts_a, core), w1, taps, long, core)).astype(BF)
    acts_a_other = swap(acts_a)
    pair = (
        lax.broadcasted_iota(jnp.int32, (long, short), 0) // 2
        == lax.broadcasted_iota(jnp.int32, (long, short), 1)
    )
    pooled = mm(mixed_a, jnp.where(pair, 0.5, 0.0).astype(BF)).astype(BF)
    pooled, ups = tie((pooled, ups))
    pooled_all = place(exchange(pooled), z)
    up_own, up_other = shifted(halo(ups, core), core, taps)
    pooled_all, acts_a_other, up_own, up_other = tie((pooled_all, acts_a_other, up_own, up_other))
    pooled_other = swap(pooled_all)
    up_recv = swap(up_other)
    widened = by_core(core, mm(ww[0], pooled_all), mm(ww[1], pooled_all)).astype(BF)
    blocks_b, pooled_other, up_recv = tie((exchange(widened), pooled_other, up_recv))
    factor_b, acts_b, sloped_b = activate(blocks_b, z)
    mixed_b = (widened.astype(F32) + conv(halo(acts_b, core), w2, taps, short, core)).astype(BF)
    blocks_c, acts_b_other = tie((exchange(mixed_b), swap(acts_b)))
    factor_c, acts_c, sloped_c = activate(blocks_c, z)
    acts_c_other = swap(acts_c)

    sent, finish = block_back(up_own, up_other, mixed_b, factor_c, sloped_c, w3, z)
    third = weight_terms([(acts_c, acts_c_other, up_own, up_recv)], x, y, None)
    got, third = tie((send_z(sent), third))
    grad_mid = ups.astype(F32) + finish(got)
    mid_spread, third = tie((halo(grad_mid.astype(BF), core), third))
    d_own, d_other = shifted(mid_spread, core, taps)
    third = send_first(third)
    sent, finish = block_back(d_own, d_other, widened, factor_b, sloped_b, w2, z)
    cut = w2[0].shape[0] // 2 // 128 * 128 + 128
    second = weight_terms([(acts_b, acts_b_other, d_own, swap(d_other))], x, y, cut)
    got, second = tie((send_z(sent), second))
    grad_top = grad_mid + finish(got)

    top_own, top_other = halves(grad_top.astype(BF), core)
    part = mm_rows(ww[0], top_own) + mm_rows(ww[1], top_other)
    got = [rot(piece(part, z, j).astype(BF), "z", j) for j in (1, 2, 3)]
    got, top_recv = tie((got, swap(top_other)))
    grad_pooled = piece(part, z, 0)
    for g in got:
        grad_pooled = grad_pooled + g.astype(F32)
    grad_mixed = lax.dot_general(
        grad_pooled,
        jnp.where(pair, 0.5, 0.0).astype(F32),
        (((1,), (1,)), ((), ())),
        precision=lax.Precision.HIGHEST,
        preferred_element_type=F32,
    )
    mixed_spread = halo(grad_mixed.astype(BF), core)
    d_own, d_other = shifted(mixed_spread, core, taps)
    sent, finish = block_back(d_own, d_other, feats, factor_a, sloped_a, w1, z)
    first = weight_terms(
        [
            (acts_a, acts_a_other, d_own, swap(d_other)),
            (pooled_all, pooled_other, top_own, top_recv),
        ],
        x,
        y,
        384,
    )
    sent, second, third = tie((sent, second, third))
    got = send_z(sent)
    second = send_first(second)
    third = reduce_last(third)
    got, second, first = tie((got, second, first))
    grad_fine = (grad_mixed + finish(got)).astype(BF)

    own, other = halves(grad_fine, core)
    grad_features = by_core(core, own, swap(other), axis=1)

    def taps_out(flat_sum):
        grp = flat_sum.shape[0]
        return (flat_sum * grad_scale).reshape(grp, taps, -1).transpose(1, 0, 2)

    last = reduce_last(send_first(first))
    cut = w1[0].shape[0]
    return (
        grad_features,
        taps_out(last[:, :cut]),
        last[:, -weight_widen.shape[0] :] * grad_scale,
        taps_out(reduce_last(second)),
        taps_out(third),
    )


def solution(mesh):
    axes = mesh.axis_names
    devices = mesh.devices
    if axes != ("seq", "chan"):
        devices = devices.T
    parts = Mesh(devices.reshape(4, 4, 4, 2), ("x", "y", "z", "core"))
    seq, chan = ("x", "y"), ("z", "core")
    placed = (
        P(chan, seq),
        P(None, chan, None),
        P(chan, None),
        P(None, chan, None),
        P(None, chan, None),
        P(chan, seq),
    )
    return jax.shard_map(
        on_device,
        mesh=parts,
        in_specs=placed,
        out_specs=(
            P(chan, seq),
            P(None, seq, chan),
            P(seq, chan),
            P(None, seq, chan),
            P(None, seq, chan),
        ),
        check_vma=False,
    )
```
